128 devices in a mesh: ctx: 128 (over y, x, z, core).
Axes of the slice: x: 4, y: 4, z: 4, core: 2. Of those that a mesh axis runs over, the one named last changes fastest.
Arguments:
- q_load: bfloat16 [131072, 1024], P('ctx'), may hold values from -16 to 16
- k_load: bfloat16 [131072, 128], P('ctx'), may hold values from -12 to 12
- v_load: bfloat16 [131072, 128], P('ctx'), may hold values from -6 to 6
- dest_row: int32 [131072], P('ctx'), may hold values from 0 to 131071, as said below
- doc_id: int32 [131072], P('ctx'), may hold values from 0 to 511, never falling along the last dimension, each value on 1 to 512 neighbouring positions
- grad_out: bfloat16 [131072, 1024], P('ctx'), may hold values from -6 to 6
Outputs:
- attended: bfloat16 [131072, 1024], P('ctx')
- grad_q: float32 [131072, 1024], P('ctx')
- grad_k: float32 [131072, 128], P('ctx')
- grad_v: float32 [131072, 128], P('ctx')
The draws below stay inside these ranges and needn't reach their ends.
Inputs may be any that keep to these rules, and one draw needn't show every extreme that they name: `dest_row`: each sequence position appears once; row j of a device's 1024 loader rows has its sequence position among the 1024 positions of device j // 8. `doc_id`: document numbers never fall along the sequence and each document has 1 to 512 tokens.
All inputs are finite; a program needn't handle non-finite values.
Results may differ from the reference program's by a relative error of at most 0.03.
Values may be sent and summed in bfloat16 or wider, within the bound.
A program may use at most 128 MiB of HBM per device.

```python
import math
import jax
import jax.numpy as jnp
import numpy as np
from jax import lax

H = 8
DH = 128
TOK_DEV = 1024
BLK = 128
MAXDOC = 512
TOKENS = 131072
PEER = 8
DOCS = 512


def draw_q_load(key, part):
    noise = jax.random.normal(jax.random.fold_in(key, 11), (TOKENS, H * DH), jnp.float32)
    result = jnp.clip(noise, -6.0, 6.0)
    return result.astype(jnp.bfloat16)


def draw_k_load(key, part):
    noise = jax.random.normal(jax.random.fold_in(key, 21), (TOKENS, DH), jnp.float32)
    result = jnp.clip(noise, -6.0, 6.0)
    return result.astype(jnp.bfloat16)


def draw_dest_row(key, part):
    count = TOKENS // TOK_DEV
    orders = jax.vmap(lambda device: jax.random.permutation(jax.random.fold_in(key, device), TOK_DEV))(jnp.arange(count))
    slots = jnp.arange(TOK_DEV)
    source = slots // PEER
    within = slots % PEER
    loader = source[None, :] * TOK_DEV + jnp.arange(count)[:, None] * PEER + within[None, :]
    target = jnp.arange(count)[:, None] * TOK_DEV + orders
    return jnp.zeros((TOKENS,), jnp.int32).at[loader.reshape(-1)].set(target.reshape(-1).astype(jnp.int32))


def shard_levels(key, shape, cuts, smallest, largest):
    factor_of, own = 1.0, jax.random.fold_in(key, 6)
    for dim, blocks in cuts:
        heights = jnp.exp(jax.random.uniform(jax.random.fold_in(own, dim), (blocks,), jnp.float32, smallest / len(cuts), largest / len(cuts)))
        factor_of = factor_of * jnp.repeat(heights, shape[dim] // blocks).reshape([-1 if axis == dim else 1 for axis in range(len(shape))])
    return factor_of


def split_up(amount, total, bound, slope):
    weights = [(1 << 20) // math.isqrt(rank ** slope) + 1 for rank in range(2, amount + 1)]
    spare, given = total - bound - (amount - 1), [1] * (amount - 1)
    while spare > 0:
        candidates = [i for i in range(amount - 1) if given[i] < bound]
        pool, left = sum([weights[i] for i in candidates]), spare
        for i in candidates:
            addition = min(bound - given[i], max(1, left * weights[i] // pool), spare)
            given[i] = given[i] + addition
            spare = spare - addition
    return np.array([bound] + given)


def ragged_sizes(rng, count, total, most, slope):
    if count == 2:
        one = jax.random.randint(rng, (), max(1, total - most), min(most, total - 1) + 1)
        return jnp.stack([one, total - one])
    lengths = jnp.asarray(split_up(count, total, most, slope), jnp.int32)
    couples = (count - 1) // 2
    donor, sink = lengths[1:1 + 2 * couples:2], lengths[2:2 + 2 * couples:2]
    slack = jnp.minimum(donor - 1, most - sink)
    passed = jax.random.randint(jax.random.fold_in(rng, 1), (couples,), 0, 1 << 20) % (slack + 1)
    lengths = lengths.at[1:1 + 2 * couples:2].set(donor - passed).at[2:2 + 2 * couples:2].set(sink + passed)
    return lengths[jax.random.permutation(jax.random.fold_in(rng, 2), count)]


def gaussian(own_key, extent, deviation, most, shards=(), held_as=jnp.bfloat16):
    level = shard_levels(own_key, extent, shards, -0.22, 0.18) if shards else 1.0
    drawn = jax.random.normal(own_key, extent, jnp.float32) * deviation * level
    return jnp.minimum(jnp.maximum(drawn, -most), most).astype(held_as)


def setup_inputs(seed: int = 0) -> dict:
    keys = jax.random.split(jax.random.key(seed), 7)
    q_load = draw_q_load(jax.random.fold_in(keys[6], 71), 0)
    k_load = draw_k_load(jax.random.fold_in(keys[6], 71), 0)
    v_load = gaussian(keys[2], (TOKENS, DH), 1.0, 6.0, ((0, 128),))
    dest_row = draw_dest_row(jax.random.fold_in(keys[6], 71), 0)
    doc_id = jnp.searchsorted(jnp.cumsum(ragged_sizes(keys[4], DOCS, TOKENS, MAXDOC, 1)), jnp.arange(TOKENS), side="right").astype(jnp.int32)
    grad_out = gaussian(keys[5], (TOKENS, H * DH), 1.0, 6.0, ((0, 128),))
    return dict(q_load=q_load, k_load=k_load, v_load=v_load, dest_row=dest_row, doc_id=doc_id, grad_out=grad_out)


masked_value = -1e+30

def tile_grads(pieces, offset, scaling):
    q_tile, k_tile, v_tile, grad_tile, q_docs, k_docs = pieces
    block_len = q_tile.shape[1]
    key_len = k_tile.shape[1]
    q_full = q_tile.astype(jnp.float32)
    k_full = k_tile.astype(jnp.float32)
    v_full = v_tile.astype(jnp.float32)
    g_full = grad_tile.astype(jnp.float32)
    scores = jnp.einsum('gihd,gjd->ghij', q_full, k_full) * scaling
    causal = jnp.arange(key_len)[None, :] - offset <= jnp.arange(block_len)[:, None]
    allowed = (q_docs[:, :, None] == k_docs[:, None, :]) & causal[None]
    scores = jnp.where(allowed[:, None], scores, masked_value)
    top_score = lax.optimization_barrier(jnp.max(scores, axis=-1, keepdims=True))
    log_total = top_score + jnp.log(lax.optimization_barrier(jnp.sum(jnp.exp(scores - top_score), axis=-1, keepdims=True)))
    soft_w = jnp.exp(scores - log_total)
    soft_b = soft_w.astype(jnp.bfloat16).astype(jnp.float32)
    attended = jnp.einsum('ghij,gjd->gihd', soft_b, v_full).astype(jnp.bfloat16)
    delta = lax.optimization_barrier(jnp.sum(g_full * attended.astype(jnp.float32), axis=-1))
    delta = jnp.transpose(delta, (0, 2, 1))[..., None]
    grad_v = jnp.einsum('ghij,gihd->gjd', soft_b, g_full)
    grad_p = jnp.einsum('gihd,gjd->ghij', g_full, v_full)
    grad_s = (soft_w * (grad_p - delta)).astype(jnp.bfloat16).astype(jnp.float32)
    grad_q = jnp.einsum('ghij,gjd->gihd', grad_s, k_full) * scaling
    grad_k = jnp.einsum('ghij,gihd->gjd', grad_s, q_full) * scaling
    return (attended, grad_q, grad_k, grad_v)

def attend(q_rows, ext_k, ext_v, ext_doc, q_doc, grad_rows, block_len, rim):
    n_rows, width = q_rows.shape
    head_dim = ext_k.shape[1]
    heads = width // head_dim
    n_blocks = n_rows // block_len
    rim_blocks = rim // block_len
    reach = rim_blocks + 1

    def windows(source):
        stacked = source.reshape((n_blocks + rim_blocks, block_len) + source.shape[1:])
        joined = jnp.stack([stacked[w:w + n_blocks] for w in range(reach)], axis=1)
        return joined.reshape((n_blocks, reach * block_len) + source.shape[1:])
    per_step = math.gcd(n_blocks, 4)
    step_count = n_blocks // per_step

    def grouped(source):
        return source.reshape((step_count, per_step) + source.shape[1:])
    pieces = (grouped(q_rows.reshape(n_blocks, block_len, heads, head_dim)), grouped(windows(ext_k)), grouped(windows(ext_v)), grouped(grad_rows.reshape(n_blocks, block_len, heads, head_dim)), grouped(q_doc.reshape(n_blocks, block_len)), grouped(windows(ext_doc)))
    scaling = 1.0 / math.sqrt(head_dim)
    attended, grad_q, grad_k, grad_v = lax.map(lambda p: tile_grads(p, rim, scaling), pieces)
    attended = attended.reshape(n_rows, width)
    grad_q = grad_q.reshape(n_rows, width)
    grad_k = grad_k.reshape(n_blocks, reach, block_len, head_dim)
    grad_v = grad_v.reshape(n_blocks, reach, block_len, head_dim)
    total_k = jnp.zeros((n_blocks + rim_blocks, block_len, head_dim), jnp.float32)
    total_v = jnp.zeros((n_blocks + rim_blocks, block_len, head_dim), jnp.float32)
    for w in range(reach):
        total_k = total_k.at[w:w + n_blocks].add(grad_k[:, w])
        total_v = total_v.at[w:w + n_blocks].add(grad_v[:, w])
    return (attended, grad_q, total_k.reshape(-1, head_dim), total_v.reshape(-1, head_dim))

def reference(q_load, k_load, v_load, dest_row, doc_id, grad_out):
    q_seq = jnp.zeros_like(q_load).at[dest_row].set(q_load)
    k_seq = jnp.zeros_like(k_load).at[dest_row].set(k_load)
    v_seq = jnp.zeros_like(v_load).at[dest_row].set(v_load)
    doc_plus = (doc_id + 1).astype(jnp.int32)
    front = jnp.zeros((MAXDOC, DH), jnp.bfloat16)
    ext_k = jnp.concatenate([front, k_seq], axis=0)
    ext_v = jnp.concatenate([front, v_seq], axis=0)
    ext_doc = jnp.concatenate([jnp.zeros((MAXDOC,), jnp.int32), doc_plus], axis=0)
    attended, grad_q, total_k, total_v = attend(q_seq, ext_k, ext_v, ext_doc, doc_plus, grad_out, BLK, MAXDOC)
    return (attended, grad_q, total_k[MAXDOC:], total_v[MAXDOC:])
```

```python
import functools
import math

import jax
import jax.numpy as jnp
from jax import lax
from jax.experimental import pallas as pl
from jax.experimental.pallas import tpu as pltpu
from jax.sharding import PartitionSpec as P

BLK = 128
MAXDOC = 512
REACH = MAXDOC // BLK
MASKED = -1e30

NT = (((1,), (1,)), ((), ()))


def dot(a, b):
    return jnp.dot(a, b, preferred_element_type=jnp.float32)


def dot_nt(a, b):
    return lax.dot_general(a, b, NT, preferred_element_type=jnp.float32)


def identity(n):
    rows = lax.broadcasted_iota(jnp.int32, (n, n), 0)
    cols = lax.broadcasted_iota(jnp.int32, (n, n), 1)
    return jnp.where(rows == cols, 1.0, 0.0).astype(jnp.bfloat16)


def passed_along(array, axis, by):
    count = lax.axis_size(axis)
    pairs = [(i, i + by) for i in range(count) if 0 <= i + by < count]
    return lax.ppermute(array, axis, pairs)


def slots_of(pos_cols):
    lane = lax.broadcasted_iota(jnp.int32, (8, BLK), 1)
    weights = jnp.where(lane == 0, 32.0, jnp.where(lane == 1, 1.0, 0.0)).astype(jnp.bfloat16)
    return dot_nt(weights, pos_cols)[0:1].astype(jnp.int32)


def selection(slots, first):
    want = first + lax.broadcasted_iota(jnp.int32, (BLK, slots.shape[1]), 0)
    return jnp.where(slots == want, 1.0, 0.0).astype(jnp.bfloat16)


def place_kernel(n_rows, recv_ref, kv_ref, slot_ref):
    slots = slots_of(recv_ref[:, 2 * BLK :])
    slot_ref[...] = jnp.broadcast_to(slots, slot_ref.shape)
    for i in range(n_rows // BLK):
        chosen = selection(slots, i * BLK)
        kv_ref[i * BLK : (i + 1) * BLK, :] = dot(chosen, recv_ref[:, : 2 * BLK]).astype(jnp.bfloat16)


def place(recv):
    n_rows = recv.shape[0]
    return pl.pallas_call(
        functools.partial(place_kernel, n_rows),
        out_shape=(
            jax.ShapeDtypeStruct((n_rows, 2 * BLK), jnp.bfloat16),
            jax.ShapeDtypeStruct((8, n_rows), jnp.int32),
        ),
        in_specs=[pl.BlockSpec(memory_space=pltpu.VMEM)],
        out_specs=(pl.BlockSpec(memory_space=pltpu.VMEM),) * 2,
        name="place_kv",
    )(recv)


def attend_kernel(
    n_blocks,
    heads,
    group,
    docs_smem,
    q_ref,
    slot_ref,
    kv_ref,
    halo_ref,
    doc_ref,
    grad_ref,
    att_ref,
    gq_ref,
    gk_ref,
    gv_ref,
    q_s,
    k_s,
    v_s,
    bias_s,
    dk_s,
    dv_s,
):
    step = pl.program_id(0)
    rim = REACH * BLK
    scale = 1.0 / math.sqrt(BLK)
    to_log2 = scale * math.log2(math.e)

    @pl.when(step == 0)
    def _():
        k_s[0:rim, :] = halo_ref[:, :BLK]
        k_s[rim:, :] = kv_ref[:, :BLK]
        v_s[0:rim, 0:BLK] = halo_ref[:, BLK:]
        v_s[rim:, 0:BLK] = kv_ref[:, BLK:]
        v_s[:, BLK:] = jnp.ones((rim + n_blocks * BLK, BLK), jnp.bfloat16)
        dk_s[...] = jnp.zeros_like(dk_s)
        dv_s[...] = jnp.zeros_like(dv_s)

    chosen = selection(slot_ref[0:1, :], step * BLK)
    q_s[...] = dot(chosen, q_ref[...]).astype(jnp.bfloat16)

    own = docs_smem[(step + REACH) * BLK]
    reach = jnp.int32(1)
    for w in range(1, REACH + 1):
        reach = reach + jnp.where(docs_smem[(step + REACH - w + 1) * BLK - 1] == own, 1, 0)

    q_docs = jnp.transpose(jnp.broadcast_to(doc_ref[pl.ds(step + REACH, 1), :], (BLK, BLK)))

    def run(n):
        width = n * BLK
        first = step + REACH + 1 - n
        start = pl.multiple_of(first * BLK, BLK)
        keys = pl.ds(start, width)
        row = lax.broadcasted_iota(jnp.int32, (BLK, BLK), 0)
        col = lax.broadcasted_iota(jnp.int32, (BLK, BLK), 1)
        for w in range(n):
            same = q_docs == doc_ref[pl.ds(first + w, 1), :]
            if w == n - 1:
                same = same & (col <= row)
            bias_s[:, w * BLK : (w + 1) * BLK] = jnp.where(same, 0.0, MASKED)
        eye = identity(BLK)
        ones = jnp.ones((BLK, BLK), jnp.bfloat16)
        rows = group * BLK

        def piece(g):
            at = [g * group * BLK + h * BLK for h in range(group)]
            q = jnp.concatenate([q_s[:, a : a + BLK] for a in at], axis=0)
            grad = jnp.concatenate([grad_ref[:, a : a + BLK] for a in at], axis=0)
            scores = dot_nt(q, k_s[keys, :]) * to_log2
            scores = (
                scores.reshape(group, BLK, width) + bias_s[:, :width][None]
            ).reshape(rows, width)
            top = jnp.max(scores, axis=-1, keepdims=True)
            weight = jnp.exp2(scores - top)
            weight_b = weight.astype(jnp.bfloat16)
            both = dot(weight_b, v_s[keys, :])
            inverse = 1.0 / both[:, BLK:]
            attended = (both[:, :BLK] * inverse).astype(jnp.bfloat16)
            grad_n = grad.astype(jnp.float32) * inverse
            product = grad_n * attended.astype(jnp.float32)
            delta = dot(product.astype(jnp.bfloat16), ones)
            grad_n = grad_n.astype(jnp.bfloat16)
            grad_p = dot_nt(grad_n, v_s[keys, 0:BLK])
            grad_s = jnp.concatenate(
                [
                    weight[:, w * BLK : (w + 1) * BLK]
                    * (grad_p[:, w * BLK : (w + 1) * BLK] - delta)
                    for w in range(n)
                ],
                axis=1,
            ).astype(jnp.bfloat16)
            grad_q = dot(grad_s, k_s[keys, :]) * scale
            for h, a in enumerate(at):
                att_ref[:, a : a + BLK] = attended[h * BLK : (h + 1) * BLK]
                gq_ref[:, a : a + BLK] = grad_q[h * BLK : (h + 1) * BLK]
            grad_t = dot_nt(eye, grad_n).astype(jnp.bfloat16)
            q_t = dot_nt(eye, q).astype(jnp.bfloat16)
            dv_s[:, keys] += dot(grad_t, weight_b)
            dk_s[:, keys] += dot(q_t, grad_s)

        for g in range(heads // group):
            piece(g)

    for n in range(1, REACH + 2):
        pl.when(reach == n)(functools.partial(run, n))

    @pl.when(step == n_blocks - 1)
    def _():
        for b in range(n_blocks + REACH):
            part = slice(b * BLK, (b + 1) * BLK)
            gk_ref[part, :] = jnp.transpose(dk_s[:, part]) * scale
            gv_ref[part, :] = jnp.transpose(dv_s[:, part])


def attend(q_recv, slots, kv_seq, halo, ext_doc, grad_out):
    n_rows, width = q_recv.shape
    heads = width // BLK
    n_blocks = n_rows // BLK
    ext = n_rows + MAXDOC
    whole = lambda shape: pl.BlockSpec(shape, lambda i, docs: (0, 0))
    per_block = pl.BlockSpec((BLK, width), lambda i, docs: (i, 0))
    return pl.pallas_call(
        functools.partial(attend_kernel, n_blocks, heads, 2),
        out_shape=(
            jax.ShapeDtypeStruct((n_rows, width), jnp.bfloat16),
            jax.ShapeDtypeStruct((n_rows, width), jnp.float32),
            jax.ShapeDtypeStruct((ext, BLK), jnp.float32),
            jax.ShapeDtypeStruct((ext, BLK), jnp.float32),
        ),
        grid_spec=pltpu.PrefetchScalarGridSpec(
            num_scalar_prefetch=1,
            grid=(n_blocks,),
            in_specs=[
                whole((n_rows, width)),
                whole((8, n_rows)),
                whole((n_rows, 2 * BLK)),
                whole((MAXDOC, 2 * BLK)),
                whole((ext // BLK, BLK)),
                per_block,
            ],
            out_specs=[per_block, per_block, whole((ext, BLK)), whole((ext, BLK))],
            scratch_shapes=[
                pltpu.VMEM((BLK, width), jnp.bfloat16),
                pltpu.VMEM((ext, BLK), jnp.bfloat16),
                pltpu.VMEM((ext, 2 * BLK), jnp.bfloat16),
                pltpu.VMEM((BLK, MAXDOC + BLK), jnp.float32),
                pltpu.VMEM((BLK, ext), jnp.float32),
                pltpu.VMEM((BLK, ext), jnp.float32),
            ],
        ),
        compiler_params=pltpu.CompilerParams(
            dimension_semantics=("arbitrary",), vmem_limit_bytes=40 << 20
        ),
        name="attend",
    )(ext_doc, q_recv, slots, kv_seq, halo, ext_doc.reshape(ext // BLK, BLK), grad_out)


def position_columns(dest_row, n_rows):
    local = (dest_row % n_rows)[:, None]
    lane = lax.broadcasted_iota(jnp.int32, (n_rows, BLK), 1)
    parts = jnp.where(lane == 0, local // 32, jnp.where(lane == 1, local % 32, 0))
    return parts.astype(jnp.bfloat16)


def exchange(array):
    return lax.all_to_all(array, "ctx", split_axis=0, concat_axis=0, tiled=True)


def body(q_load, k_load, v_load, dest_row, doc_id, grad_out):
    n_rows, width = q_load.shape
    doc_plus = doc_id + 1
    prev_doc = passed_along(doc_plus[n_rows - MAXDOC :], "ctx", 1)
    ext_doc = jnp.concatenate([prev_doc, doc_plus])
    recv_kv = exchange(
        jnp.concatenate([k_load, v_load, position_columns(dest_row, n_rows)], axis=1)
    )
    recv_q = exchange(q_load)
    kv_seq, slots = place(recv_kv)
    halo = passed_along(kv_seq[n_rows - MAXDOC :], "ctx", 1)
    attended, grad_q, total_k, total_v = attend(
        recv_q, slots, kv_seq, halo, ext_doc, grad_out
    )
    back = passed_along(
        jnp.concatenate([total_k[:MAXDOC], total_v[:MAXDOC]], axis=1).astype(jnp.bfloat16),
        "ctx",
        -1,
    ).astype(jnp.float32)
    padding = ((n_rows - MAXDOC, 0), (0, 0))
    grad_k = total_k[MAXDOC:] + jnp.pad(back[:, :BLK], padding)
    grad_v = total_v[MAXDOC:] + jnp.pad(back[:, BLK:], padding)
    return (attended, grad_q, grad_k, grad_v)


def solution(mesh):
    in_specs = (P("ctx", None), P("ctx", None), P("ctx", None), P("ctx"), P("ctx"), P("ctx", None))
    out_specs = (P("ctx", None), P("ctx", None), P("ctx", None), P("ctx", None))
    return jax.shard_map(body, mesh=mesh, in_specs=in_specs, out_specs=out_specs, check_vma=False)
```
